32 devices in a mesh: row: 8 (over y, x, core), col: 4 (over z).
Axes of the slice: x: 2, y: 2, z: 4, core: 2. Of those that a mesh axis runs over, the one named last changes fastest.
Arguments:
- attn_out: bfloat16 [2, 256, 16384], P(None, 'row', 'col'), may hold values from -6 to 6
- o_weight: bfloat16 [16384, 16384], P('col', 'row'), may hold values from -0.046875 to 0.046875
- residual: float32 [2, 256, 16384], P(None, 'col', 'row'), may hold values from -73 to 73
- norm_gain: float32 [16384], replicated, may hold values from 0.5 to 1.5
- gram_in: float32 [16384, 16384], P('row', 'col'), may hold values from -0.1 to 1.5
Outputs:
- gram: float32 [16384, 16384], P('row', 'col')
The draws below stay inside these ranges and needn't reach their ends.
All inputs are finite; a program needn't handle non-finite values.
Results may differ from the reference program's by a relative error of at most 0.0003.
Values may be sent and summed in bfloat16 or wider, within the bound.
A program may use at most 192 MiB of HBM per device.

```python
import math
import jax
import jax.numpy as jnp
from jax import lax

D = 16384
GROUPS = 2
CT = 256


def draw_residual(key, part):
    subkeys = jax.random.split(key, 4)
    feature_ramp = jnp.exp(math.log(3.0) * jnp.arange(D, dtype=jnp.float32) / D)
    feature_rough = jnp.exp(jax.random.uniform(subkeys[0], (D,), jnp.float32, -0.69, 0.69))
    token_scale = jnp.exp(jax.random.uniform(subkeys[1], (GROUPS, CT, 1), jnp.float32, math.log(0.3), math.log(3.0)))
    entries = jnp.clip(jax.random.normal(subkeys[3], (GROUPS, CT, D), jnp.float32), -4.0, 4.0)
    return entries * token_scale * (feature_ramp * feature_rough)[None, None, :]


def draw_gram_in(key, part):
    subkeys = jax.random.split(jax.random.fold_in(key, 7), 2)
    diag_values = jax.random.uniform(subkeys[0], (D,), jnp.float32, 0.5, 1.5)
    off_values = jnp.clip(0.02 * jax.random.normal(subkeys[1], (D, D), jnp.float32), -0.1, 0.1)
    row_ids = jnp.arange(D, dtype=jnp.int32)
    on_diag = row_ids[:, None] == row_ids[None, :]
    return jnp.where(on_diag, diag_values[:, None], off_values)


def levels(rng, extent, shards, smallest, largest):
    def one(position, blocks):
        heights = jax.random.uniform(jax.random.fold_in(jax.random.fold_in(rng, 6), position), (blocks,), jnp.float32, smallest / len(shards), largest / len(shards))
        return jnp.repeat(jnp.exp(heights), extent[position] // blocks).reshape((-1,) + (1,) * (len(extent) - position - 1))

    loudness = one(*shards[0])
    for cut in shards[1:]:
        loudness = loudness * one(*cut)
    return loudness


def normal_values(stream_key, shape, scale, limit, cuts=(), held_as=jnp.bfloat16):
    level = levels(stream_key, shape, cuts, -0.22, 0.18) if cuts else 1.0
    values = jax.random.normal(stream_key, shape, jnp.float32) * scale * level
    return jnp.minimum(jnp.maximum(values, -limit), limit).astype(held_as)


def setup_inputs(seed: int = 0) -> dict:
    splits = jax.random.split(jax.random.key(seed), 6)
    attn_out = normal_values(splits[0], (GROUPS, CT, D), 1.0, 6.0, ((1, 8), (2, 4)))
    o_weight = normal_values(splits[1], (D, D), D ** -0.5, 0.046875, ((0, 4), (1, 8)))
    residual = draw_residual(jax.random.fold_in(splits[5], 71), 0)
    norm_gain = jnp.clip(1.0 + 0.1 * jax.random.normal(splits[3], (D,), jnp.float32), 0.5, 1.5)
    gram_in = draw_gram_in(jax.random.fold_in(splits[5], 71), 0)
    return {"attn_out": attn_out, "o_weight": o_weight, "residual": residual, "norm_gain": norm_gain, "gram_in": gram_in}


epsilon_norm = 1e-05
highest = lax.Precision.HIGHEST

def reference(attn_out, o_weight, residual, norm_gain, gram_in):
    weight_wide = o_weight.astype(jnp.float32)
    gram_sum = jnp.zeros((D, D), jnp.float32)
    for block_index in range(GROUPS):
        projected = jnp.dot(attn_out[block_index].astype(jnp.float32), weight_wide, precision=highest, preferred_element_type=jnp.float32)
        stream = projected + residual[block_index]
        mean_square = lax.optimization_barrier(jnp.mean(stream * stream, axis=1, keepdims=True))
        normed = stream * lax.rsqrt(mean_square + epsilon_norm) * norm_gain[None, :]
        gram_sum = gram_sum + lax.dot_general(normed, normed, (((0,), (0,)), ((), ())), precision=highest, preferred_element_type=jnp.float32)
    return gram_in + gram_sum / (GROUPS * CT)
```

```python
import functools

import jax
import jax.numpy as jnp
from jax import lax
from jax.experimental import pallas as pl
from jax.experimental.pallas import tpu as pltpu
from jax.sharding import PartitionSpec as P

epsilon_norm = 1e-05
MESH = pl.DeviceIdType.MESH
f8 = jnp.float8_e4m3fn
f32 = jnp.float32
bf16 = jnp.bfloat16
PIECE = 16
TOP = 2.0 ** 7.4
TINY = 1e-30
LOW = 2.0 ** 8
HOP = 3
RING_HOP = 3


def power17(v):
    v2 = v * v
    v4 = v2 * v2
    v8 = v4 * v4
    return v8 * v8 * v


def root17(y):
    y = y.astype(f32)
    return y * jnp.exp2(jnp.log2(jnp.maximum(jnp.abs(y), 1e-37)) * (-16.0 / 17.0))


def pack(values, first):
    lane = lax.broadcasted_iota(jnp.int32, (8, 128), 1)
    out = jnp.zeros((8, 128), f32)
    for r in range(values.shape[0] // 8):
        out = jnp.where(lane == first + r, values[8 * r:8 * r + 8], out)
    return out


def spread(packed, count, width):
    return jnp.concatenate([jnp.broadcast_to(packed[:, r:r + 1], (8, width)) for r in range(count)], axis=0)


def remote(src, dst, send_sem, recv_sem, row, col):
    return pltpu.make_async_remote_copy(
        src_ref=src, dst_ref=dst, send_sem=send_sem, recv_sem=recv_sem,
        device_id=(row, col), device_id_type=MESH)


def operands_kernel(rows, cols, fan, model, attn_ref, w_ref, res_ref, gain_row, gain_col,
                    lt_hi, lt8, r_hi, r8,
                    attn, wbuf, own, st, z_out, z_in, zs_out, zs_in, cp, stats,
                    w_sem, loc_sem, at_send, at_fwd, at_recv, z_send, z_recv, zs_send, zs_recv,
                    ring_send, mate_send, cp_recv, st_send, st_recv):
    me = lax.axis_index("row")
    col = lax.axis_index("col")
    chips = rows // fan
    chip, core = me // fan, me % fan
    last = cols - 1
    blocks, bt = attn.shape[0], attn.shape[1]
    per, tw = wbuf.shape[0], wbuf.shape[2]
    tiles = blocks * per
    lanes_per = bt // 8
    tokens = blocks * bt
    groups, tile = res_ref.shape[0], res_ref.shape[1] // fan

    order = [j ^ (j >> 1) for j in range(chips)]
    ahead = jnp.int32(0)
    behind = jnp.int32(0)
    spot = jnp.int32(0)
    source_spot = jnp.int32(0)
    for j in range(chips):
        spot = jnp.where(chip == order[j], j, spot)
        source_spot = jnp.where(col == order[j], j, source_spot)
        ahead = jnp.where(chip == order[j], order[(j + 1) % chips], ahead)
        behind = jnp.where(chip == order[j], order[(j + chips - 1) % chips], behind)
    to_chip = jnp.where(core % 2 == 0, ahead, behind)
    to_row = to_chip * fan + core
    is_source = chip == col
    feeds_ring = to_chip != col
    turn = jnp.where(core % 2 == 0, spot - source_spot, source_spot - spot)
    ring_hops = (turn + chips) % chips

    def weight_copy(s):
        return pltpu.make_async_copy(w_ref.at[:, pl.ds(pl.multiple_of(s * tw, tw), tw)], wbuf.at[s], w_sem.at[s])

    def start_weights(s, carry):
        weight_copy(s).start()
        return carry

    lax.fori_loop(0, per, start_weights, 0)

    barrier = pltpu.get_barrier_semaphore()
    for off in range(1, rows):
        pl.semaphore_signal(barrier, inc=1, device_id=((me + off) % rows, col), device_id_type=MESH)

    @pl.when(col > 0)
    def _():
        pl.semaphore_signal(barrier, inc=1, device_id=(me, col - 1), device_id_type=MESH)

    @pl.when(col < last)
    def _():
        pl.semaphore_signal(barrier, inc=1, device_id=(me, col + 1), device_id_type=MESH)

    pl.semaphore_wait(barrier, rows - 1 + jnp.minimum(col, 1) + jnp.minimum(last - col, 1))

    def piece(b, row):
        return attn.at[b, pl.ds(pl.multiple_of(row * PIECE, PIECE), PIECE)]

    def mine(b):
        return attn_ref.at[pl.ds(pl.multiple_of(b * PIECE, PIECE), PIECE)]

    def attn_local(b):
        return pltpu.make_async_copy(mine(b), piece(b, me), loc_sem.at[b])

    def attn_far(b, off):
        there = ((chip + off) % chips) * fan + core
        return remote(mine(b), piece(b, me), at_send.at[b, off], at_recv.at[b, me], there, col)

    def attn_mate(b, off, other):
        mate = chip * fan + (core + other) % fan
        slot = ((chip + chips - off) % chips) * fan + core
        src = mine(b) if off == 0 else piece(b, slot)
        return remote(src, piece(b, slot), at_fwd.at[b, off, other], at_recv.at[b, slot], mate, col)

    def attn_arrive(b, slot):
        remote(mine(b), piece(b, slot), at_send.at[b, 0], at_recv.at[b, slot], me, col).wait_recv()

    def attn_start(b):
        attn_local(b).start()
        for other in range(1, fan):
            attn_mate(b, 0, other).start()
        for off in range(1, chips):
            attn_far(b, off).start()

    def attn_forward(b):
        for off in range(1, chips):
            attn_arrive(b, ((chip + chips - off) % chips) * fan + core)
            for other in range(1, fan):
                attn_mate(b, off, other).start()

    def attn_finish(b):
        attn_local(b).wait()
        for off in range(chips):
            for other in range(1, fan):
                attn_arrive(b, ((chip + chips - off) % chips) * fan + (core + other) % fan)

    attn_start(0)
    attn_forward(0)
    if blocks > 1:
        attn_start(1)

    def z_copy(d, i):
        nxt = jnp.minimum(col + 1, last) if d == 0 else jnp.maximum(col - 1, 0)
        return remote(z_out.at[d, i], z_in.at[d, i], z_send.at[d, i], z_recv.at[d, i], me, nxt)

    def zs_copy(d, i):
        nxt = jnp.minimum(col + 1, last) if d == 0 else jnp.maximum(col - 1, 0)
        return remote(zs_out.at[d, i], zs_in.at[d, i], zs_send.at[d, i], zs_recv.at[d, i], me, nxt)

    def z_decode(d, i):
        return root17(z_in[d, i]) * spread(zs_in[d, i], lanes_per, tw)

    def z_encode(d, i, value):
        top = jnp.maximum(jnp.max(jnp.abs(value), axis=1, keepdims=True), TINY)
        z_out[d, i] = power17(value * (TOP / top)).astype(bf16)
        zs_out[d, i] = pack(top * (1.0 / TOP), 0)
        zs_copy(d, i).start()
        z_copy(d, i).start()

    def lanes(which):
        return pl.ds(pl.multiple_of(which * 128, 128), 128)

    def ring_copy(i):
        return remote(cp.at[core, i], cp.at[core, i], ring_send.at[i], cp_recv.at[core, i], to_row, col)

    def mate_copy(i, other):
        mate = chip * fan + (core + other) % fan
        return remote(cp.at[core, i], cp.at[core, i], mate_send.at[other, i], cp_recv.at[core, i], mate, col)

    def cp_arrive(which, i):
        remote(cp.at[which, i], cp.at[which, i], ring_send.at[i], cp_recv.at[which, i], me, col).wait_recv()

    def stat_copy(b, off):
        return remote(stats.at[me, b], stats.at[me, b], st_send.at[off, b], st_recv.at[me, b], (me + off) % rows, col)

    def stat_arrive(b, off):
        there = (me + off) % rows
        remote(stats.at[there, b], stats.at[there, b], st_send.at[off, b], st_recv.at[there, b], me, col).wait_recv()

    far = jnp.maximum(col, last - col)

    def combine(i):
        @pl.when(col > 0)
        def _():
            own[i] = own[i] + z_decode(0, i)

        @pl.when(col < last)
        def _():
            own[i] = own[i] + z_decode(1, i)

        b, s = i // per, i % per
        total = own[i]
        square = jnp.sum(total * total, axis=1, keepdims=True)
        packed = pack(square, s * lanes_per)

        @pl.when(s == 0)
        def _():
            stats[me, b] = packed

        @pl.when(s > 0)
        def _():
            stats[me, b] = stats[me, b] + packed

        st[i] = (total * gain_row[0, s]).T

        @pl.when(is_source)
        def _():
            cp[core, i] = power17(total * (lax.rsqrt(square + TINY) * TOP)).astype(bf16)
            ring_copy(i).start()
            for other in range(1, fan):
                mate_copy(i, other).start()

        @pl.when(s == per - 1)
        def _():
            for off in range(1, rows):
                stat_copy(b, off).start()

    def finish(b):
        for off in range(1, rows):
            stat_arrive(b, off)
        total = stats[0, b]
        for r in range(1, rows):
            total = total + stats[r, b]
        panel = stats[col * fan, b]
        for k in range(1, fan):
            panel = panel + stats[col * fan + k, b]
        shift = 64
        while shift >= lanes_per:
            total = total + pltpu.roll(total, shift, axis=1)
            panel = panel + pltpu.roll(panel, shift, axis=1)
            shift //= 2
        panel = panel * (1.0 / (fan * per * tw)) + TINY
        level = lax.rsqrt(panel)
        weight = panel * level / (total * (1.0 / model) + epsilon_norm)
        along = spread(weight, lanes_per, 128).T
        along = jnp.broadcast_to(along[:1, :], (tw, bt))
        here = pl.ds(pl.multiple_of(b * bt, bt), bt)
        there = pl.ds(pl.multiple_of(tokens + b * bt, bt), bt)

        def left(s, carry):
            value = st[b * per + s] * along
            high = value.astype(bf16)
            low = value - high.astype(f32)
            at = pl.ds(pl.multiple_of(s * tw, tw), tw)
            lt_hi[at, here] = high
            lt8[at, here] = value.astype(f8)
            lt8[at, there] = (low * LOW).astype(f8)
            return carry

        lax.fori_loop(0, per, left, 0)

        for k in range(fan):
            norm = jnp.sqrt(stats[col * fan + k, b] + TINY) * (1.0 / TOP)

            def right(s, carry, k=k, norm=norm):
                i = b * per + s

                @pl.when(k != core)
                def _():
                    cp_arrive(k, i)

                scale = pltpu.roll(norm, (128 - s * lanes_per) % 128, axis=1) * level
                value = root17(cp[k, i]) * spread(scale, lanes_per, tw) * gain_col[0, k * per + s]
                high = value.astype(bf16)
                low = value - high.astype(f32)
                at = pl.ds(pl.multiple_of((k * per + s) * tw, tw), tw)
                r_hi[here, at] = high
                r8[here, at] = (low * LOW).astype(f8)
                r8[there, at] = value.astype(f8)
                return carry

            lax.fori_loop(0, per, right, 0)

    def step(t, carry):
        @pl.when(t < tiles)
        def _():
            b, s = t // per, t % per

            @pl.when(s == 0)
            def _():
                attn_finish(b)

            @pl.when(b == 0)
            def _():
                weight_copy(s).wait()

            own[t] = jnp.dot(attn[b], wbuf[s], preferred_element_type=f32)
            at = pl.ds(pl.multiple_of(s * tw, tw), tw)
            g = (b * PIECE) // tile
            for f in range(fan):
                here = pl.ds(pl.multiple_of((col * fan + f) * PIECE, PIECE), PIECE)
                there = pl.ds(pl.multiple_of(f * tile + (b * PIECE) % tile, PIECE), PIECE)
                own[t, here, :] = own[t, here, :] + res_ref[g, there, at]

            @pl.when(jnp.logical_and(s == per // 2, b + 1 < blocks))
            def _():
                attn_forward(b + 1)

                @pl.when(b + 2 < blocks)
                def _():
                    attn_start(b + 2)

        for d in range(2):
            hops = col if d == 0 else last - col
            i = t - HOP * hops

            @pl.when(jnp.logical_and(i >= 0, i < tiles))
            def _(d=d, hops=hops, i=i):
                @pl.when(hops == 0)
                def _():
                    z_encode(d, i, own[i])

                @pl.when(hops > 0)
                def _():
                    zs_copy(d, i).wait_recv()
                    z_copy(d, i).wait_recv()

                @pl.when(jnp.logical_and(hops > 0, hops < last))
                def _():
                    z_encode(d, i, own[i] + z_decode(d, i))

        i = t - HOP * far

        @pl.when(jnp.logical_and(i >= 0, i < tiles))
        def _(i=i):
            combine(i)

        i = t - HOP * far - RING_HOP * ring_hops

        @pl.when(jnp.logical_and(ring_hops > 0, jnp.logical_and(i >= 0, i < tiles)))
        def _(i=i):
            cp_arrive(core, i)

            @pl.when(feeds_ring)
            def _():
                ring_copy(i).start()

            for other in range(1, fan):
                mate_copy(i, other).start()

        i = t - HOP * far - RING_HOP * (chips - 1) - 1

        @pl.when(jnp.logical_and(i >= 0, jnp.logical_and(i < tiles, i % per == per - 1)))
        def _(i=i):
            finish(i // per)

        return carry

    lax.fori_loop(0, tiles + HOP * far + RING_HOP * (chips - 1) + 1, step, 0)

    def drain(i, carry):
        for other in range(1, fan):
            mate_copy(i, other).wait_send()

        @pl.when(jnp.logical_or(is_source, feeds_ring))
        def _():
            ring_copy(i).wait_send()

        for d in range(2):
            @pl.when(col != (last if d == 0 else 0))
            def _(d=d):
                z_copy(d, i).wait_send()
                zs_copy(d, i).wait_send()
        return carry

    lax.fori_loop(0, tiles, drain, 0)

    def drain_block(b, carry):
        for off in range(1, rows):
            stat_copy(b, off).wait_send()
        for off in range(chips):
            for other in range(1, fan):
                attn_mate(b, off, other).wait_send()
        for off in range(1, chips):
            attn_far(b, off).wait_send()
        return carry

    lax.fori_loop(0, blocks, drain_block, 0)


def operands(attn, weights, residual, gain_row, gain_col, rows, cols, fan):
    own_tokens, depth = attn.shape
    width = weights.shape[1]
    model = width * rows
    blocks = own_tokens // PIECE
    bt = rows * PIECE
    tokens = blocks * bt
    per = 128 // (bt // 8)
    tw = width // per
    tiles = blocks * per
    chips = rows // fan
    vmem = pl.BlockSpec(memory_space=pltpu.VMEM)
    hbm = pl.BlockSpec(memory_space=pl.ANY)
    dma = pltpu.SemaphoreType.DMA
    return pl.pallas_call(
        functools.partial(operands_kernel, rows, cols, fan, model),
        out_shape=(
            jax.ShapeDtypeStruct((width, tokens), bf16),
            jax.ShapeDtypeStruct((width, 2 * tokens), f8),
            jax.ShapeDtypeStruct((tokens, fan * width), bf16),
            jax.ShapeDtypeStruct((2 * tokens, fan * width), f8),
        ),
        in_specs=[hbm, hbm, vmem, vmem, vmem],
        out_specs=(vmem, vmem, vmem, vmem),
        scratch_shapes=[
            pltpu.VMEM((blocks, bt, depth), bf16),
            pltpu.VMEM((per, depth, tw), bf16),
            pltpu.VMEM((tiles, bt, tw), f32),
            pltpu.VMEM((tiles, tw, bt), f32),
            pltpu.VMEM((2, tiles, bt, tw), bf16),
            pltpu.VMEM((2, tiles, bt, tw), bf16),
            pltpu.VMEM((2, tiles, 8, 128), f32),
            pltpu.VMEM((2, tiles, 8, 128), f32),
            pltpu.VMEM((fan, tiles, bt, tw), bf16),
            pltpu.VMEM((rows, blocks, 8, 128), f32),
            dma((per,)), dma((blocks,)),
            dma((blocks, chips)), dma((blocks, chips, fan)), dma((blocks, rows)),
            dma((2, tiles)), dma((2, tiles)), dma((2, tiles)), dma((2, tiles)),
            dma((tiles,)), dma((fan, tiles)), dma((fan, tiles)),
            dma((rows, blocks)), dma((rows, blocks)),
        ],
        compiler_params=pltpu.CompilerParams(collective_id=0, has_side_effects=True, vmem_limit_bytes=60 << 20),
        name="operands",
    )(attn, weights, residual, gain_row.reshape(1, per, 1, tw), gain_col.reshape(1, fan * per, 1, tw))


def gram_kernel(tokens, step, lt_hi, lt8, r_hi, r8, gram_in, out):
    height, panel = out.shape
    here = pl.ds(pl.multiple_of(pl.program_id(0) * height, height), height)
    for j in range(panel // step):
        at = slice(j * step, (j + 1) * step)
        low = jnp.dot(lt8[here, :], r8[:, at], preferred_element_type=f32)
        high = jnp.dot(lt_hi[here, :], r_hi[:, at], preferred_element_type=f32)
        out[:, at] = gram_in[:, at] + (high + low * (1.0 / LOW)) * (1.0 / tokens)


def gram_product(lt_hi, lt8, r_hi, r8, gram_in):
    model_rows, panel = gram_in.shape
    tokens = r_hi.shape[0]
    height = 256
    vmem = pl.BlockSpec(memory_space=pltpu.VMEM)
    block = pl.BlockSpec((height, panel), lambda i: (i, 0))
    return pl.pallas_call(
        functools.partial(gram_kernel, tokens, 512),
        grid=(model_rows // height,),
        out_shape=jax.ShapeDtypeStruct(gram_in.shape, f32),
        in_specs=[vmem, vmem, vmem, vmem, block],
        out_specs=block,
        compiler_params=pltpu.CompilerParams(vmem_limit_bytes=40 << 20),
        name="gram_product",
    )(lt_hi, lt8, r_hi, r8, gram_in)


def body(attn_out, o_weight, residual, norm_gain, gram_in):
    rows = lax.axis_size("row")
    cols = lax.axis_size("col")
    fan = rows // cols
    width = o_weight.shape[1]
    gain_row = lax.dynamic_slice_in_dim(norm_gain, lax.axis_index("row") * width, width)
    gain_col = lax.dynamic_slice_in_dim(norm_gain, lax.axis_index("col") * fan * width, fan * width)
    parts = operands(attn_out.reshape(-1, attn_out.shape[2]), o_weight, residual, gain_row, gain_col, rows, cols, fan)
    return gram_product(*parts, gram_in)


def solution(mesh):
    return jax.shard_map(
        body,
        mesh=mesh,
        in_specs=(
            P(None, "row", "col"),
            P("col", "row"),
            P(None, "col", "row"),
            P(),
            P("row", "col"),
        ),
        out_specs=P("row", "col"),
        check_vma=False,
    )
```

```python
import functools

import jax
import jax.numpy as jnp
from jax import lax
from jax.experimental import pallas as pl
from jax.experimental.pallas import tpu as pltpu
from jax.sharding import PartitionSpec as P

epsilon_norm = 1e-05
MESH = pl.DeviceIdType.MESH
f8 = jnp.float8_e4m3fn
f32 = jnp.float32
bf16 = jnp.bfloat16
PIECE = 16
TOP = 2.0 ** 7.4
TINY = 1e-30
LOW = 2.0 ** 8
HOP = 4
SLOTS = 8
RING_HOP = 4


def power17(v):
    v2 = v * v
    v4 = v2 * v2
    v8 = v4 * v4
    return v8 * v8 * v


def root17(y):
    y = y.astype(f32)
    return y * jnp.exp2(jnp.log2(jnp.maximum(jnp.abs(y), 1e-37)) * (-16.0 / 17.0))


def pack(values, first):
    lane = lax.broadcasted_iota(jnp.int32, (8, 128), 1)
    out = jnp.zeros((8, 128), f32)
    for r in range(values.shape[0] // 8):
        out = jnp.where(lane == first + r, values[8 * r:8 * r + 8], out)
    return out


def spread(packed, count, width):
    return jnp.concatenate([jnp.broadcast_to(packed[:, r:r + 1], (8, width)) for r in range(count)], axis=0)


def remote(src, dst, send_sem, recv_sem, row, col):
    return pltpu.make_async_remote_copy(
        src_ref=src, dst_ref=dst, send_sem=send_sem, recv_sem=recv_sem,
        device_id=(row, col), device_id_type=MESH)


def operands_kernel(rows, cols, fan, model, attn_ref, w_ref, res_hbm, gain_hbm,
                    lt_hi, lt8, r_hi, r8,
                    res_ref, gain, attn, wbuf, own, st, z_out, z_in, zs_out, zs_in, cp, stats, cscale,
                    w_sem, in_sem, loc_sem, at_send, at_fwd, at_recv, z_send, z_recv, zs_send, zs_recv,
                    ring_send, mate_send, cp_recv, st_send, st_recv):
    me = lax.axis_index("row")
    col = lax.axis_index("col")
    chips = rows // fan
    chip, core = me // fan, me % fan
    last = cols - 1
    blocks, bt = attn.shape[0], attn.shape[1]
    per, tw = wbuf.shape[0], wbuf.shape[2]
    tiles = blocks * per
    lanes_per = bt // 8
    tokens = blocks * bt
    groups, tile = res_ref.shape[0], res_ref.shape[1] // fan

    order = [j ^ (j >> 1) for j in range(chips)]
    ahead = jnp.int32(0)
    behind = jnp.int32(0)
    spot = jnp.int32(0)
    source_spot = jnp.int32(0)
    for j in range(chips):
        spot = jnp.where(chip == order[j], j, spot)
        source_spot = jnp.where(col == order[j], j, source_spot)
        ahead = jnp.where(chip == order[j], order[(j + 1) % chips], ahead)
        behind = jnp.where(chip == order[j], order[(j + chips - 1) % chips], behind)
    to_chip = jnp.where(core % 2 == 0, ahead, behind)
    to_row = to_chip * fan + core
    is_source = chip == col
    feeds_ring = to_chip != col
    turn = jnp.where(core % 2 == 0, spot - source_spot, source_spot - spot)
    ring_hops = (turn + chips) % chips

    def weight_copy(s):
        return pltpu.make_async_copy(w_ref.at[:, pl.ds(pl.multiple_of(s * tw, tw), tw)], wbuf.at[s], w_sem.at[s])

    def start_weights(s, carry):
        weight_copy(s).start()
        return carry

    res_copy = pltpu.make_async_copy(res_hbm, res_ref, in_sem.at[0])
    gain_copy = pltpu.make_async_copy(gain_hbm, gain, in_sem.at[1])
    res_copy.start()
    gain_copy.start()
    lax.fori_loop(0, per, start_weights, 0)

    barrier = pltpu.get_barrier_semaphore()
    for off in range(1, rows):
        pl.semaphore_signal(barrier, inc=1, device_id=((me + off) % rows, col), device_id_type=MESH)

    @pl.when(col > 0)
    def _():
        pl.semaphore_signal(barrier, inc=1, device_id=(me, col - 1), device_id_type=MESH)

    @pl.when(col < last)
    def _():
        pl.semaphore_signal(barrier, inc=1, device_id=(me, col + 1), device_id_type=MESH)

    pl.semaphore_wait(barrier, rows - 1 + jnp.minimum(col, 1) + jnp.minimum(last - col, 1))

    def piece(b, row):
        return attn.at[b, pl.ds(pl.multiple_of(row * PIECE, PIECE), PIECE)]

    def mine(b):
        return attn_ref.at[pl.ds(pl.multiple_of(b * PIECE, PIECE), PIECE)]

    def attn_local(b):
        return pltpu.make_async_copy(mine(b), piece(b, me), loc_sem.at[b])

    def attn_far(b, off):
        there = ((chip + off) % chips) * fan + core
        return remote(mine(b), piece(b, me), at_send.at[b, off], at_recv.at[b, me], there, col)

    def attn_mate(b, off, other):
        mate = chip * fan + (core + other) % fan
        slot = ((chip + chips - off) % chips) * fan + core
        src = mine(b) if off == 0 else piece(b, slot)
        return remote(src, piece(b, slot), at_fwd.at[b, off, other], at_recv.at[b, slot], mate, col)

    def attn_arrive(b, slot):
        remote(mine(b), piece(b, slot), at_send.at[b, 0], at_recv.at[b, slot], me, col).wait_recv()

    def attn_start(b):
        attn_local(b).start()
        for other in range(1, fan):
            attn_mate(b, 0, other).start()
        for off in range(1, chips):
            attn_far(b, off).start()

    def attn_forward(b):
        for off in range(1, chips):
            attn_arrive(b, ((chip + chips - off) % chips) * fan + core)
            for other in range(1, fan):
                attn_mate(b, off, other).start()

    def attn_finish(b):
        attn_local(b).wait()
        for off in range(chips):
            for other in range(1, fan):
                attn_arrive(b, ((chip + chips - off) % chips) * fan + (core + other) % fan)

    stats[me] = jnp.zeros(stats.shape[1:], f32)
    attn_start(0)
    res_copy.wait()
    gain_copy.wait()
    attn_forward(0)
    if blocks > 1:
        attn_start(1)

    def z_copy(d, i):
        nxt = jnp.minimum(col + 1, last) if d == 0 else jnp.maximum(col - 1, 0)
        return remote(z_out.at[d, i % SLOTS], z_in.at[d, i], z_send.at[d, i], z_recv.at[d, i], me, nxt)

    def zs_copy(d, i):
        nxt = jnp.minimum(col + 1, last) if d == 0 else jnp.maximum(col - 1, 0)
        return remote(zs_out.at[d, i], zs_in.at[d, i], zs_send.at[d, i], zs_recv.at[d, i], me, nxt)

    def z_decode(d, i):
        return root17(z_in[d, i]) * spread(zs_in[d, i], lanes_per, tw)

    def z_free(d, i):
        @pl.when(i >= SLOTS)
        def _():
            z_copy(d, i - SLOTS).wait_send()

    def z_encode(d, i, value):
        top = jnp.maximum(jnp.max(jnp.abs(value), axis=1, keepdims=True), TINY)
        z_out[d, i % SLOTS] = power17(value * (TOP / top)).astype(bf16)
        zs_out[d, i] = pack(top * (1.0 / TOP), 0)

    def z_start(d, i):
        zs_copy(d, i).start()
        z_copy(d, i).start()

    def z_arrive(d, i):
        zs_copy(d, i).wait_recv()
        z_copy(d, i).wait_recv()

    def lanes(which):
        return pl.ds(pl.multiple_of(which * 128, 128), 128)

    def ring_copy(i):
        return remote(cp.at[core, i], cp.at[core, i], ring_send.at[i], cp_recv.at[core, i], to_row, col)

    def mate_copy(i, other):
        mate = chip * fan + (core + other) % fan
        return remote(cp.at[core, i], cp.at[core, i], mate_send.at[other, i], cp_recv.at[core, i], mate, col)

    def cp_arrive(which, i):
        remote(cp.at[which, i], cp.at[which, i], ring_send.at[i], cp_recv.at[which, i], me, col).wait_recv()

    def stat_copy(b, off):
        return remote(stats.at[me, b], stats.at[me, b], st_send.at[off, b], st_recv.at[me, b], (me + off) % rows, col)

    def stat_arrive(b, off):
        there = (me + off) % rows
        remote(stats.at[there, b], stats.at[there, b], st_send.at[off, b], st_recv.at[there, b], me, col).wait_recv()

    far = jnp.maximum(col, last - col)
    inner = jnp.logical_and(col > 0, col < last)
    right_lag = max(per + 2, RING_HOP * (chips - 1) + 1)

    def combine(i):
        b, s = i // per, i % per

        @pl.when(col == 0)
        def _():
            gathered(i, b, s, own[i] + z_decode(1, i))

        @pl.when(inner)
        def _():
            gathered(i, b, s, own[i] + z_decode(0, i) + z_decode(1, i))

        @pl.when(col == last)
        def _():
            gathered(i, b, s, own[i] + z_decode(0, i))

        @pl.when(is_source)
        def _():
            ring_copy(i).start()
            for other in range(1, fan):
                mate_copy(i, other).start()

        @pl.when(s == per - 1)
        def _():
            for off in range(1, rows):
                stat_copy(b, off).start()

    def gathered(i, b, s, total):
        square = jnp.sum(total * total, axis=1, keepdims=True)
        stats[me, b] = jnp.where(s == 0, 0.0, stats[me, b]) + pack(square, s * lanes_per)
        st[i] = (total * gain[me * per + s]).T

        @pl.when(is_source)
        def _():
            cp[core, i] = power17(total * (lax.rsqrt(square + TINY) * TOP)).astype(bf16)

    def over_tiles(packed):
        shift = 64
        while shift >= lanes_per:
            packed = packed + pltpu.roll(packed, shift, axis=1)
            shift //= 2
        return packed

    def left(b):
        for off in range(1, rows):
            stat_arrive(b, off)
        total = stats[0, b]
        for r in range(1, rows):
            total = total + stats[r, b]
        panel = stats[col * fan, b]
        for k in range(1, fan):
            panel = panel + stats[col * fan + k, b]
        panel = over_tiles(panel) * (1.0 / (fan * per * tw)) + TINY
        level = lax.rsqrt(panel)
        for k in range(fan):
            cscale[k, b] = jnp.sqrt(stats[col * fan + k, b] + TINY) * level * (1.0 / TOP)
        weight = panel * level / (over_tiles(total) * (1.0 / model) + epsilon_norm)
        along = spread(weight, lanes_per, 128).T
        along = jnp.broadcast_to(along[:1, :], (tw, bt))
        here = pl.ds(pl.multiple_of(b * bt, bt), bt)
        there = pl.ds(pl.multiple_of(tokens + b * bt, bt), bt)

        def one(s, carry):
            value = st[b * per + s] * along
            high = value.astype(bf16)
            low = value - high.astype(f32)
            at = pl.ds(pl.multiple_of(s * tw, tw), tw)
            lt_hi[at, here] = high
            lt8[at, here] = value.astype(f8)
            lt8[at, there] = (low * LOW).astype(f8)
            return carry

        lax.fori_loop(0, per, one, 0)

    def right(i):
        b, s = i // per, i % per
        here = pl.ds(pl.multiple_of(b * bt, bt), bt)
        there = pl.ds(pl.multiple_of(tokens + b * bt, bt), bt)
        for other in range(1, fan):
            cp_arrive((core + other) % fan, i)
        for k in range(fan):
            scale = pltpu.roll(cscale[k, b], (128 - s * lanes_per) % 128, axis=1)
            value = root17(cp[k, i]) * spread(scale, lanes_per, tw) * gain[(col * fan + k) * per + s]
            high = value.astype(bf16)
            low = value - high.astype(f32)
            at = pl.ds(pl.multiple_of((k * per + s) * tw, tw), tw)
            r_hi[here, at] = high
            r8[here, at] = (low * LOW).astype(f8)
            r8[there, at] = value.astype(f8)

    def step(t, carry):
        @pl.when(t < tiles)
        def _():
            b, s = t // per, t % per

            @pl.when(s == 0)
            def _():
                attn_finish(b)

            @pl.when(b == 0)
            def _():
                weight_copy(s).wait()

            own[t] = jnp.dot(attn[b], wbuf[s], preferred_element_type=f32)
            at = pl.ds(pl.multiple_of(s * tw, tw), tw)
            g = (b * PIECE) // tile
            for f in range(fan):
                here = pl.ds(pl.multiple_of((col * fan + f) * PIECE, PIECE), PIECE)
                there = pl.ds(pl.multiple_of(f * tile + (b * PIECE) % tile, PIECE), PIECE)
                own[t, here, :] = own[t, here, :] + res_ref[g, there, at]

            @pl.when(jnp.logical_and(s == per // 2, b + 1 < blocks))
            def _():
                attn_forward(b + 1)

                @pl.when(b + 2 < blocks)
                def _():
                    attn_start(b + 2)

        up, down = t - HOP * col, t - HOP * (last - col)
        up_on = jnp.logical_and(up >= 0, up < tiles)
        down_on = jnp.logical_and(down >= 0, down < tiles)
        pair = jnp.logical_and(inner, jnp.logical_and(up_on, down_on))

        @pl.when(pair)
        def _():
            for d, i in ((0, up), (1, down)):
                z_free(d, i)
                z_arrive(d, i)
            values = [own[i] + z_decode(d, i) for d, i in ((0, up), (1, down))]
            for d, i in ((0, up), (1, down)):
                z_encode(d, i, values[d])
            for d, i in ((0, up), (1, down)):
                z_start(d, i)

        for d, i, on in ((0, up, up_on), (1, down, down_on)):
            first = col == (0 if d == 0 else last)
            end = col == (last if d == 0 else 0)

            @pl.when(jnp.logical_and(first, on))
            def _(d=d, i=i):
                z_free(d, i)
                z_encode(d, i, own[i])
                z_start(d, i)

            @pl.when(jnp.logical_and(end, on))
            def _(d=d, i=i):
                z_arrive(d, i)

            @pl.when(jnp.logical_and(jnp.logical_and(inner, on), jnp.logical_not(pair)))
            def _(d=d, i=i):
                z_free(d, i)
                z_arrive(d, i)
                z_encode(d, i, own[i] + z_decode(d, i))
                z_start(d, i)

        i = t - HOP * far

        @pl.when(jnp.logical_and(i >= 0, i < tiles))
        def _(i=i):
            combine(i)

        i = t - HOP * far - RING_HOP * ring_hops

        @pl.when(jnp.logical_and(ring_hops > 0, jnp.logical_and(i >= 0, i < tiles)))
        def _(i=i):
            cp_arrive(core, i)

            @pl.when(feeds_ring)
            def _():
                ring_copy(i).start()

            for other in range(1, fan):
                mate_copy(i, other).start()

        i = t - HOP * far - 2

        @pl.when(jnp.logical_and(i >= 0, jnp.logical_and(i < tiles, i % per == per - 1)))
        def _(i=i):
            left(i // per)

        i = t - HOP * far - right_lag

        @pl.when(jnp.logical_and(i >= 0, i < tiles))
        def _(i=i):
            right(i)

        return carry

    lax.fori_loop(0, tiles + HOP * far + right_lag, step, 0)

    def drain(i, carry):
        for other in range(1, fan):
            mate_copy(i, other).wait_send()

        @pl.when(jnp.logical_or(is_source, feeds_ring))
        def _():
            ring_copy(i).wait_send()

        for d in range(2):
            @pl.when(col != (last if d == 0 else 0))
            def _(d=d):
                zs_copy(d, i).wait_send()

                @pl.when(i >= tiles - SLOTS)
                def _():
                    z_copy(d, i).wait_send()
        return carry

    lax.fori_loop(0, tiles, drain, 0)

    def drain_block(b, carry):
        for off in range(1, rows):
            stat_copy(b, off).wait_send()
        for off in range(chips):
            for other in range(1, fan):
                attn_mate(b, off, other).wait_send()
        for off in range(1, chips):
            attn_far(b, off).wait_send()
        return carry

    lax.fori_loop(0, blocks, drain_block, 0)


def operands(attn, weights, residual, gain, rows, cols, fan):
    own_tokens, depth = attn.shape
    width = weights.shape[1]
    model = width * rows
    blocks = own_tokens // PIECE
    bt = rows * PIECE
    tokens = blocks * bt
    per = 128 // (bt // 8)
    tw = width // per
    tiles = blocks * per
    chips = rows // fan
    vmem = pl.BlockSpec(memory_space=pltpu.VMEM)
    hbm = pl.BlockSpec(memory_space=pltpu.HBM)
    dma = pltpu.SemaphoreType.DMA
    return pl.pallas_call(
        functools.partial(operands_kernel, rows, cols, fan, model),
        out_shape=(
            jax.ShapeDtypeStruct((width, tokens), bf16),
            jax.ShapeDtypeStruct((width, 2 * tokens), f8),
            jax.ShapeDtypeStruct((tokens, fan * width), bf16),
            jax.ShapeDtypeStruct((2 * tokens, fan * width), f8),
        ),
        in_specs=[hbm, hbm, hbm, hbm],
        out_specs=(vmem, vmem, vmem, vmem),
        scratch_shapes=[
            pltpu.VMEM(residual.shape, f32),
            pltpu.VMEM((rows * per, 1, tw), f32),
            pltpu.VMEM((blocks, bt, depth), bf16),
            pltpu.VMEM((per, depth, tw), bf16),
            pltpu.VMEM((tiles, bt, tw), f32),
            pltpu.VMEM((tiles, tw, bt), f32),
            pltpu.VMEM((2, SLOTS, bt, tw), bf16),
            pltpu.VMEM((2, tiles, bt, tw), bf16),
            pltpu.VMEM((2, tiles, 8, 128), f32),
            pltpu.VMEM((2, tiles, 8, 128), f32),
            pltpu.VMEM((fan, tiles, bt, tw), bf16),
            pltpu.VMEM((rows, blocks, 8, 128), f32),
            pltpu.VMEM((fan, blocks, 8, 128), f32),
            dma((per,)), dma((2,)), dma((blocks,)),
            dma((blocks, chips)), dma((blocks, chips, fan)), dma((blocks, rows)),
            dma((2, tiles)), dma((2, tiles)), dma((2, tiles)), dma((2, tiles)),
            dma((tiles,)), dma((fan, tiles)), dma((fan, tiles)),
            dma((rows, blocks)), dma((rows, blocks)),
        ],
        compiler_params=pltpu.CompilerParams(collective_id=0, has_side_effects=True, vmem_limit_bytes=40 << 20),
        name="operands",
    )(attn, weights, residual, gain.reshape(rows * per, 1, tw))


def gram_kernel(tokens, step, lt_hi, lt8, r_hi, r8, gram_in, out, total, in_sem, out_sem):
    chunks, pieces = in_sem.shape
    height, width = total.shape[0] // chunks, total.shape[1] // pieces

    def window(c, p):
        return pl.ds(pl.multiple_of(c * height, height), height), pl.ds(p * width, width)

    def load(c, p):
        return pltpu.make_async_copy(gram_in.at[window(c, p)], total.at[window(c, p)], in_sem.at[c, p])

    def store(c, p):
        return pltpu.make_async_copy(total.at[window(c, p)], out.at[window(c, p)], out_sem.at[c, p])

    def start(c, carry):
        for p in range(pieces):
            load(c, p).start()
        return carry

    def compute(c, carry):
        here = window(c, 0)[0]
        for p in range(pieces):
            load(c, p).wait()
            for j in range(width // step):
                at = slice(p * width + j * step, p * width + (j + 1) * step)
                low = jnp.dot(lt8[here, :], r8[:, at], preferred_element_type=f32)
                high = jnp.dot(lt_hi[here, :], r_hi[:, at], preferred_element_type=f32)
                total[here, at] = total[here, at] + (high + low * (1.0 / LOW)) * (1.0 / tokens)
            store(c, p).start()
        return carry

    def finish(c, carry):
        for p in range(pieces):
            store(c, p).wait()
        return carry

    lax.fori_loop(0, chunks, start, 0)
    lax.fori_loop(0, chunks, compute, 0)
    lax.fori_loop(0, chunks, finish, 0)


def gram_product(lt_hi, lt8, r_hi, r8, gram_in):
    tokens = r_hi.shape[0]
    chunks, pieces = gram_in.shape[0] // 256, gram_in.shape[1] // 1024
    vmem = pl.BlockSpec(memory_space=pltpu.VMEM)
    hbm = pl.BlockSpec(memory_space=pltpu.HBM)
    return pl.pallas_call(
        functools.partial(gram_kernel, tokens, 512),
        out_shape=jax.ShapeDtypeStruct(gram_in.shape, f32),
        in_specs=[vmem, vmem, vmem, vmem, hbm],
        out_specs=hbm,
        scratch_shapes=[
            pltpu.VMEM(gram_in.shape, f32),
            pltpu.SemaphoreType.DMA((chunks, pieces)),
            pltpu.SemaphoreType.DMA((chunks, pieces)),
        ],
        compiler_params=pltpu.CompilerParams(vmem_limit_bytes=36 << 20),
        name="gram_product",
    )(lt_hi, lt8, r_hi, r8, gram_in)


def body(attn_out, o_weight, residual, norm_gain, gram_in):
    rows = lax.axis_size("row")
    cols = lax.axis_size("col")
    fan = rows // cols
    parts = operands(attn_out.reshape(-1, attn_out.shape[2]), o_weight, residual, norm_gain, rows, cols, fan)
    return gram_product(*parts, gram_in)


def solution(mesh):
    return jax.shard_map(
        body,
        mesh=mesh,
        in_specs=(
            P(None, "row", "col"),
            P("col", "row"),
            P(None, "col", "row"),
            P(),
            P("row", "col"),
        ),
        out_specs=P("row", "col"),
        check_vma=False,
    )
```

```python
import functools

import jax
import jax.numpy as jnp
from jax import lax
from jax.experimental import pallas as pl
from jax.experimental.pallas import tpu as pltpu
from jax.sharding import PartitionSpec as P

epsilon_norm = 1e-05
MESH = pl.DeviceIdType.MESH
f8 = jnp.float8_e4m3fn
f32 = jnp.float32
bf16 = jnp.bfloat16
PIECE = 16
TOP = 2.0 ** 7.4
TINY = 1e-30
LOW = 2.0 ** 8
HOP = 4
SLOTS = 8
WEIGHTS = 3
HEIGHT = 512
RING_HOP = 4


def power17(v):
    v2 = v * v
    v4 = v2 * v2
    v8 = v4 * v4
    return v8 * v8 * v


def root17(y):
    y = y.astype(f32)
    return y * jnp.exp2(jnp.log2(jnp.maximum(jnp.abs(y), 1e-37)) * (-16.0 / 17.0))


def pack(values, first):
    lane = lax.broadcasted_iota(jnp.int32, (8, 128), 1)
    out = jnp.zeros((8, 128), f32)
    for r in range(values.shape[0] // 8):
        out = jnp.where(lane == first + r, values[8 * r:8 * r + 8], out)
    return out


def spread(packed, count, width):
    return jnp.concatenate([jnp.broadcast_to(packed[:, r:r + 1], (8, width)) for r in range(count)], axis=0)


def remote(src, dst, send_sem, recv_sem, row, col):
    return pltpu.make_async_remote_copy(
        src_ref=src, dst_ref=dst, send_sem=send_sem, recv_sem=recv_sem,
        device_id=(row, col), device_id_type=MESH)


def operands_kernel(rows, cols, fan, model, attn_ref, w_ref, res_hbm, gain_hbm, gram_in,
                    lt_hi, lt8, r_hi, r8, early,
                    res_ref, gain, attn, wbuf, own, st, z_out, z_in, zs_out, zs_in, cp, stats, cscale,
                    w_sem, in_sem, loc_sem, at_send, at_fwd, at_recv, z_send, z_recv, zs_send, zs_recv,
                    ring_send, mate_send, cp_recv, st_send, st_recv):
    me = lax.axis_index("row")
    col = lax.axis_index("col")
    chips = rows // fan
    chip, core = me // fan, me % fan
    last = cols - 1
    blocks, bt = attn.shape[0], attn.shape[1]
    ring, tw = wbuf.shape[0], wbuf.shape[2]
    per = gain.shape[0] // rows
    tiles = blocks * per
    lanes_per = bt // 8
    tokens = blocks * bt
    groups, tile = res_ref.shape[0], res_ref.shape[1] // fan

    order = [j ^ (j >> 1) for j in range(chips)]
    ahead = jnp.int32(0)
    behind = jnp.int32(0)
    spot = jnp.int32(0)
    source_spot = jnp.int32(0)
    for j in range(chips):
        spot = jnp.where(chip == order[j], j, spot)
        source_spot = jnp.where(col == order[j], j, source_spot)
        ahead = jnp.where(chip == order[j], order[(j + 1) % chips], ahead)
        behind = jnp.where(chip == order[j], order[(j + chips - 1) % chips], behind)
    to_chip = jnp.where(core % 2 == 0, ahead, behind)
    to_row = to_chip * fan + core
    is_source = chip == col
    feeds_ring = to_chip != col
    turn = jnp.where(core % 2 == 0, spot - source_spot, source_spot - spot)
    ring_hops = (turn + chips) % chips

    def weight_copy(t):
        at = pl.ds(pl.multiple_of((t % per) * tw, tw), tw)
        return pltpu.make_async_copy(w_ref.at[:, at], wbuf.at[t % ring], w_sem.at[t % ring])

    def start_weights(s, carry):
        weight_copy(s).start()
        return carry

    res_copy = pltpu.make_async_copy(res_hbm, res_ref, in_sem.at[0])
    gain_copy = pltpu.make_async_copy(gain_hbm, gain, in_sem.at[1])
    early_copy = pltpu.make_async_copy(gram_in.at[pl.ds(0, early.shape[0])], early, in_sem.at[2])
    res_copy.start()
    gain_copy.start()
    lax.fori_loop(0, ring, start_weights, 0)

    barrier = pltpu.get_barrier_semaphore()
    for off in range(1, rows):
        pl.semaphore_signal(barrier, inc=1, device_id=((me + off) % rows, col), device_id_type=MESH)

    @pl.when(col > 0)
    def _():
        pl.semaphore_signal(barrier, inc=1, device_id=(me, col - 1), device_id_type=MESH)

    @pl.when(col < last)
    def _():
        pl.semaphore_signal(barrier, inc=1, device_id=(me, col + 1), device_id_type=MESH)

    pl.semaphore_wait(barrier, rows - 1 + jnp.minimum(col, 1) + jnp.minimum(last - col, 1))

    def piece(b, row):
        return attn.at[b, pl.ds(pl.multiple_of(row * PIECE, PIECE), PIECE)]

    def mine(b):
        return attn_ref.at[pl.ds(pl.multiple_of(b * PIECE, PIECE), PIECE)]

    def attn_local(b):
        return pltpu.make_async_copy(mine(b), piece(b, me), loc_sem.at[b])

    def attn_far(b, off):
        there = ((chip + off) % chips) * fan + core
        return remote(mine(b), piece(b, me), at_send.at[b, off], at_recv.at[b, me], there, col)

    def attn_mate(b, off, other):
        mate = chip * fan + (core + other) % fan
        slot = ((chip + chips - off) % chips) * fan + core
        src = mine(b) if off == 0 else piece(b, slot)
        return remote(src, piece(b, slot), at_fwd.at[b, off, other], at_recv.at[b, slot], mate, col)

    def attn_arrive(b, slot):
        remote(mine(b), piece(b, slot), at_send.at[b, 0], at_recv.at[b, slot], me, col).wait_recv()

    def attn_start(b):
        attn_local(b).start()
        for other in range(1, fan):
            attn_mate(b, 0, other).start()
        for off in range(1, chips):
            attn_far(b, off).start()

    def attn_forward(b):
        for off in range(1, chips):
            attn_arrive(b, ((chip + chips - off) % chips) * fan + core)
            for other in range(1, fan):
                attn_mate(b, off, other).start()

    def attn_finish(b):
        attn_local(b).wait()
        for off in range(chips):
            for other in range(1, fan):
                attn_arrive(b, ((chip + chips - off) % chips) * fan + (core + other) % fan)

    stats[me] = jnp.zeros(stats.shape[1:], f32)
    attn_start(0)
    res_copy.wait()
    gain_copy.wait()
    attn_forward(0)
    if blocks > 1:
        attn_start(1)

    def z_copy(d, i):
        nxt = jnp.minimum(col + 1, last) if d == 0 else jnp.maximum(col - 1, 0)
        return remote(z_out.at[d, i % SLOTS], z_in.at[d, i], z_send.at[d, i], z_recv.at[d, i], me, nxt)

    def zs_copy(d, i):
        nxt = jnp.minimum(col + 1, last) if d == 0 else jnp.maximum(col - 1, 0)
        return remote(zs_out.at[d, i], zs_in.at[d, i], zs_send.at[d, i], zs_recv.at[d, i], me, nxt)

    def z_decode(d, i):
        return root17(z_in[d, i]) * spread(zs_in[d, i], lanes_per, tw)

    def z_free(d, i):
        @pl.when(i >= SLOTS)
        def _():
            z_copy(d, i - SLOTS).wait_send()

    def z_encode(d, i, value):
        top = jnp.maximum(jnp.max(jnp.abs(value), axis=1, keepdims=True), TINY)
        z_out[d, i % SLOTS] = power17(value * (TOP / top)).astype(bf16)
        zs_out[d, i] = pack(top * (1.0 / TOP), 0)

    def z_start(d, i):
        zs_copy(d, i).start()
        z_copy(d, i).start()

    def z_arrive(d, i):
        zs_copy(d, i).wait_recv()
        z_copy(d, i).wait_recv()

    def lanes(which):
        return pl.ds(pl.multiple_of(which * 128, 128), 128)

    def ring_copy(i):
        return remote(cp.at[core, i], cp.at[core, i], ring_send.at[i], cp_recv.at[core, i], to_row, col)

    def mate_copy(i, other):
        mate = chip * fan + (core + other) % fan
        return remote(cp.at[core, i], cp.at[core, i], mate_send.at[other, i], cp_recv.at[core, i], mate, col)

    def cp_arrive(which, i):
        remote(cp.at[which, i], cp.at[which, i], ring_send.at[i], cp_recv.at[which, i], me, col).wait_recv()

    def stat_copy(b, off):
        return remote(stats.at[me, b], stats.at[me, b], st_send.at[off, b], st_recv.at[me, b], (me + off) % rows, col)

    def stat_arrive(b, off):
        there = (me + off) % rows
        remote(stats.at[there, b], stats.at[there, b], st_send.at[off, b], st_recv.at[there, b], me, col).wait_recv()

    far = jnp.maximum(col, last - col)
    inner = jnp.logical_and(col > 0, col < last)
    right_lag = max(per + 2, RING_HOP * (chips - 1) + 1)

    def combine(i):
        b, s = i // per, i % per

        @pl.when(col == 0)
        def _():
            gathered(i, b, s, own[i] + z_decode(1, i))

        @pl.when(inner)
        def _():
            gathered(i, b, s, own[i] + z_decode(0, i) + z_decode(1, i))

        @pl.when(col == last)
        def _():
            gathered(i, b, s, own[i] + z_decode(0, i))

        @pl.when(is_source)
        def _():
            ring_copy(i).start()
            for other in range(1, fan):
                mate_copy(i, other).start()

        @pl.when(s == per - 1)
        def _():
            for off in range(1, rows):
                stat_copy(b, off).start()

    def gathered(i, b, s, total):
        square = jnp.sum(total * total, axis=1, keepdims=True)
        stats[me, b] = jnp.where(s == 0, 0.0, stats[me, b]) + pack(square, s * lanes_per)
        st[i] = (total * gain[me * per + s]).T

        @pl.when(is_source)
        def _():
            cp[core, i] = power17(total * (lax.rsqrt(square + TINY) * TOP)).astype(bf16)

    def over_tiles(packed):
        shift = 64
        while shift >= lanes_per:
            packed = packed + pltpu.roll(packed, shift, axis=1)
            shift //= 2
        return packed

    def left(b):
        for off in range(1, rows):
            stat_arrive(b, off)
        total = stats[0, b]
        for r in range(1, rows):
            total = total + stats[r, b]
        panel = stats[col * fan, b]
        for k in range(1, fan):
            panel = panel + stats[col * fan + k, b]
        panel = over_tiles(panel) * (1.0 / (fan * per * tw)) + TINY
        level = lax.rsqrt(panel)
        for k in range(fan):
            cscale[k, b] = jnp.sqrt(stats[col * fan + k, b] + TINY) * level * (1.0 / TOP)
        weight = panel * level / (over_tiles(total) * (1.0 / model) + epsilon_norm)
        along = spread(weight, lanes_per, 128).T
        along = jnp.broadcast_to(along[:1, :], (tw, bt))
        here = pl.ds(pl.multiple_of(b * bt, bt), bt)
        there = pl.ds(pl.multiple_of(tokens + b * bt, bt), bt)

        def one(s, carry):
            value = st[b * per + s] * along
            high = value.astype(bf16)
            low = value - high.astype(f32)
            at = pl.ds(pl.multiple_of(s * tw, tw), tw)
            lt_hi[at, here] = high
            lt8[at, here] = value.astype(f8)
            lt8[at, there] = (low * LOW).astype(f8)
            return carry

        lax.fori_loop(0, per, one, 0)

    def right(i):
        b, s = i // per, i % per
        here = pl.ds(pl.multiple_of(b * bt, bt), bt)
        there = pl.ds(pl.multiple_of(tokens + b * bt, bt), bt)
        for other in range(1, fan):
            cp_arrive((core + other) % fan, i)
        for k in range(fan):
            scale = pltpu.roll(cscale[k, b], (128 - s * lanes_per) % 128, axis=1)
            value = root17(cp[k, i]) * spread(scale, lanes_per, tw) * gain[(col * fan + k) * per + s]
            high = value.astype(bf16)
            low = value - high.astype(f32)
            at = pl.ds(pl.multiple_of((k * per + s) * tw, tw), tw)
            r_hi[here, at] = high
            r8[here, at] = (low * LOW).astype(f8)
            r8[there, at] = value.astype(f8)

    def step(t, carry):
        @pl.when(t < tiles)
        def _():
            b, s = t // per, t % per

            @pl.when(s == 0)
            def _():
                attn_finish(b)

            weight_copy(t).wait()
            own[t] = jnp.dot(attn[b], wbuf[t % ring], preferred_element_type=f32)

            @pl.when(t + ring < tiles)
            def _():
                weight_copy(t + ring).start()

            @pl.when(t == per)
            def _():
                early_copy.start()

            at = pl.ds(pl.multiple_of(s * tw, tw), tw)
            g = (b * PIECE) // tile
            for f in range(fan):
                here = pl.ds(pl.multiple_of((col * fan + f) * PIECE, PIECE), PIECE)
                there = pl.ds(pl.multiple_of(f * tile + (b * PIECE) % tile, PIECE), PIECE)
                own[t, here, :] = own[t, here, :] + res_ref[g, there, at]

            @pl.when(jnp.logical_and(s == per // 2, b + 1 < blocks))
            def _():
                attn_forward(b + 1)

                @pl.when(b + 2 < blocks)
                def _():
                    attn_start(b + 2)

        up, down = t - HOP * col, t - HOP * (last - col)
        up_on = jnp.logical_and(up >= 0, up < tiles)
        down_on = jnp.logical_and(down >= 0, down < tiles)
        pair = jnp.logical_and(inner, jnp.logical_and(up_on, down_on))

        @pl.when(pair)
        def _():
            for d, i in ((0, up), (1, down)):
                z_free(d, i)
                z_arrive(d, i)
            values = [own[i] + z_decode(d, i) for d, i in ((0, up), (1, down))]
            for d, i in ((0, up), (1, down)):
                z_encode(d, i, values[d])
            for d, i in ((0, up), (1, down)):
                z_start(d, i)

        for d, i, on in ((0, up, up_on), (1, down, down_on)):
            first = col == (0 if d == 0 else last)
            end = col == (last if d == 0 else 0)

            @pl.when(jnp.logical_and(first, on))
            def _(d=d, i=i):
                z_free(d, i)
                z_encode(d, i, own[i])
                z_start(d, i)

            @pl.when(jnp.logical_and(end, on))
            def _(d=d, i=i):
                z_arrive(d, i)

            @pl.when(jnp.logical_and(jnp.logical_and(inner, on), jnp.logical_not(pair)))
            def _(d=d, i=i):
                z_free(d, i)
                z_arrive(d, i)
                z_encode(d, i, own[i] + z_decode(d, i))
                z_start(d, i)

        i = t - HOP * far

        @pl.when(jnp.logical_and(i >= 0, i < tiles))
        def _(i=i):
            combine(i)

        i = t - HOP * far - RING_HOP * ring_hops

        @pl.when(jnp.logical_and(ring_hops > 0, jnp.logical_and(i >= 0, i < tiles)))
        def _(i=i):
            cp_arrive(core, i)

            @pl.when(feeds_ring)
            def _():
                ring_copy(i).start()

            for other in range(1, fan):
                mate_copy(i, other).start()

        i = t - HOP * far - 2

        @pl.when(jnp.logical_and(i >= 0, jnp.logical_and(i < tiles, i % per == per - 1)))
        def _(i=i):
            left(i // per)

        i = t - HOP * far - right_lag

        @pl.when(jnp.logical_and(i >= 0, i < tiles))
        def _(i=i):
            right(i)

        return carry

    lax.fori_loop(0, tiles + HOP * far + right_lag, step, 0)

    early_copy.wait()

    def drain(i, carry):
        for other in range(1, fan):
            mate_copy(i, other).wait_send()

        @pl.when(jnp.logical_or(is_source, feeds_ring))
        def _():
            ring_copy(i).wait_send()

        for d in range(2):
            @pl.when(col != (last if d == 0 else 0))
            def _(d=d):
                zs_copy(d, i).wait_send()

                @pl.when(i >= tiles - SLOTS)
                def _():
                    z_copy(d, i).wait_send()
        return carry

    lax.fori_loop(0, tiles, drain, 0)

    def drain_block(b, carry):
        for off in range(1, rows):
            stat_copy(b, off).wait_send()
        for off in range(chips):
            for other in range(1, fan):
                attn_mate(b, off, other).wait_send()
        for off in range(1, chips):
            attn_far(b, off).wait_send()
        return carry

    lax.fori_loop(0, blocks, drain_block, 0)


def operands(attn, weights, residual, gain, gram_in, early, rows, cols, fan):
    own_tokens, depth = attn.shape
    width = weights.shape[1]
    model = width * rows
    blocks = own_tokens // PIECE
    bt = rows * PIECE
    tokens = blocks * bt
    per = 128 // (bt // 8)
    tw = width // per
    tiles = blocks * per
    chips = rows // fan
    vmem = pl.BlockSpec(memory_space=pltpu.VMEM)
    hbm = pl.BlockSpec(memory_space=pltpu.HBM)
    dma = pltpu.SemaphoreType.DMA
    return pl.pallas_call(
        functools.partial(operands_kernel, rows, cols, fan, model),
        out_shape=(
            jax.ShapeDtypeStruct((width, tokens), bf16),
            jax.ShapeDtypeStruct((width, 2 * tokens), f8),
            jax.ShapeDtypeStruct((tokens, fan * width), bf16),
            jax.ShapeDtypeStruct((2 * tokens, fan * width), f8),
            jax.ShapeDtypeStruct((early, gram_in.shape[1]), f32),
        ),
        in_specs=[hbm, hbm, hbm, hbm, hbm],
        out_specs=(vmem, vmem, vmem, vmem, vmem),
        scratch_shapes=[
            pltpu.VMEM(residual.shape, f32),
            pltpu.VMEM((rows * per, 1, tw), f32),
            pltpu.VMEM((blocks, bt, depth), bf16),
            pltpu.VMEM((WEIGHTS, depth, tw), bf16),
            pltpu.VMEM((tiles, bt, tw), f32),
            pltpu.VMEM((tiles, tw, bt), f32),
            pltpu.VMEM((2, SLOTS, bt, tw), bf16),
            pltpu.VMEM((2, tiles, bt, tw), bf16),
            pltpu.VMEM((2, tiles, 8, 128), f32),
            pltpu.VMEM((2, tiles, 8, 128), f32),
            pltpu.VMEM((fan, tiles, bt, tw), bf16),
            pltpu.VMEM((rows, blocks, 8, 128), f32),
            pltpu.VMEM((fan, blocks, 8, 128), f32),
            dma((WEIGHTS,)), dma((3,)), dma((blocks,)),
            dma((blocks, chips)), dma((blocks, chips, fan)), dma((blocks, rows)),
            dma((2, tiles)), dma((2, tiles)), dma((2, tiles)), dma((2, tiles)),
            dma((tiles,)), dma((fan, tiles)), dma((fan, tiles)),
            dma((rows, blocks)), dma((rows, blocks)),
        ],
        compiler_params=pltpu.CompilerParams(collective_id=0, has_side_effects=True, vmem_limit_bytes=31 << 20),
        name="operands",
    )(attn, weights, residual, gain.reshape(rows * per, 1, tw), gram_in)


def gram_kernel(tokens, step, lt_hi, lt8, r_hi, r8, early, gram_in, out, total, in_sem, out_sem):
    chunks, pieces = in_sem.shape
    height, width = total.shape[0] // chunks, total.shape[1] // pieces

    def window(c, p):
        return pl.ds(pl.multiple_of(c * height, height), height), pl.ds(p * width, width)

    def load(c, p):
        return pltpu.make_async_copy(gram_in.at[window(c, p)], total.at[window(c, p)], in_sem.at[c, p])

    def store(c, p):
        return pltpu.make_async_copy(total.at[window(c, p)], out.at[window(c, p)], out_sem.at[c, p])

    def start(c, carry):
        for p in range(pieces):
            load(c, p).start()
        return carry

    def product(c, p, begin):
        here = window(c, 0)[0]
        for j in range(width // step):
            at = slice(p * width + j * step, p * width + (j + 1) * step)
            low = jnp.dot(lt8[here, :], r8[:, at], preferred_element_type=f32)
            high = jnp.dot(lt_hi[here, :], r_hi[:, at], preferred_element_type=f32)
            total[here, at] = begin(here, at) + (high + low * (1.0 / LOW)) * (1.0 / tokens)
        store(c, p).start()

    def compute(c, carry):
        for p in range(pieces):
            load(c, p).wait()
            product(c, p, lambda here, at: total[here, at])
        return carry

    def finish(c, carry):
        for p in range(pieces):
            store(c, p).wait()
        return carry

    lax.fori_loop(1, chunks, start, 0)
    for p in range(pieces):
        product(0, p, lambda here, at: early[:, at])
    lax.fori_loop(1, chunks, compute, 0)
    lax.fori_loop(0, chunks, finish, 0)


def gram_product(lt_hi, lt8, r_hi, r8, early, gram_in):
    tokens = r_hi.shape[0]
    chunks, pieces = gram_in.shape[0] // HEIGHT, gram_in.shape[1] // 1024
    vmem = pl.BlockSpec(memory_space=pltpu.VMEM)
    hbm = pl.BlockSpec(memory_space=pltpu.HBM)
    return pl.pallas_call(
        functools.partial(gram_kernel, tokens, 256),
        out_shape=jax.ShapeDtypeStruct(gram_in.shape, f32),
        in_specs=[vmem, vmem, vmem, vmem, vmem, hbm],
        out_specs=hbm,
        scratch_shapes=[
            pltpu.VMEM(gram_in.shape, f32),
            pltpu.SemaphoreType.DMA((chunks, pieces)),
            pltpu.SemaphoreType.DMA((chunks, pieces)),
        ],
        compiler_params=pltpu.CompilerParams(vmem_limit_bytes=33 << 20),
        name="gram_product",
    )(lt_hi, lt8, r_hi, r8, early, gram_in)


def body(attn_out, o_weight, residual, norm_gain, gram_in):
    rows = lax.axis_size("row")
    cols = lax.axis_size("col")
    fan = rows // cols
    parts = operands(attn_out.reshape(-1, attn_out.shape[2]), o_weight, residual, norm_gain, gram_in, HEIGHT, rows, cols, fan)
    return gram_product(*parts, gram_in)


def solution(mesh):
    return jax.shard_map(
        body,
        mesh=mesh,
        in_specs=(
            P(None, "row", "col"),
            P("col", "row"),
            P(None, "col", "row"),
            P(),
            P("row", "col"),
        ),
        out_specs=P("row", "col"),
        check_vma=False,
    )
```

```python
import functools

import jax
import jax.numpy as jnp
from jax import lax
from jax.experimental import pallas as pl
from jax.experimental.pallas import tpu as pltpu
from jax.sharding import PartitionSpec as P

epsilon_norm = 1e-05
MESH = pl.DeviceIdType.MESH
f8 = jnp.float8_e4m3fn
f32 = jnp.float32
bf16 = jnp.bfloat16
PIECE = 16
TOP = 2.0 ** 7.4
TINY = 1e-30
LOW = 2.0 ** 8
HOP = 6
SLOTS = 8
WEIGHTS = 3
HEIGHT = 512
RING_HOP = 4


def power17(v):
    v2 = v * v
    v4 = v2 * v2
    v8 = v4 * v4
    return v8 * v8 * v


def root17(y):
    y = y.astype(f32)
    return y * jnp.exp2(jnp.log2(jnp.maximum(jnp.abs(y), 1e-37)) * (-16.0 / 17.0))


def pack(values, first):
    lane = lax.broadcasted_iota(jnp.int32, (8, 128), 1)
    out = jnp.zeros((8, 128), f32)
    for r in range(values.shape[0] // 8):
        out = jnp.where(lane == first + r, values[8 * r:8 * r + 8], out)
    return out


def spread(packed, count, width):
    return jnp.concatenate([jnp.broadcast_to(packed[:, r:r + 1], (8, width)) for r in range(count)], axis=0)


def remote(src, dst, send_sem, recv_sem, row, col):
    return pltpu.make_async_remote_copy(
        src_ref=src, dst_ref=dst, send_sem=send_sem, recv_sem=recv_sem,
        device_id=(row, col), device_id_type=MESH)


def operands_kernel(rows, cols, fan, model, attn_ref, w_ref, res_hbm, gain_hbm, gram_in,
                    lt_hi, lt8, r_hi, r8, early,
                    res_ref, gain, attn, wbuf, own, st, z_out, z_in, zs_out, zs_in, cp, stats, cscale,
                    w_sem, in_sem, loc_sem, at_send, at_fwd, at_recv, z_send, z_recv, zs_send, zs_recv,
                    ring_send, mate_send, cp_recv, st_send, st_recv):
    me = lax.axis_index("row")
    col = lax.axis_index("col")
    chips = rows // fan
    chip, core = me // fan, me % fan
    last = cols - 1
    blocks, bt = attn.shape[0], attn.shape[1]
    ring, tw = wbuf.shape[0], wbuf.shape[2]
    per = gain.shape[0] // rows
    tiles = blocks * per
    lanes_per = bt // 8
    tokens = blocks * bt
    groups, tile = res_ref.shape[0], res_ref.shape[1] // fan

    order = [j ^ (j >> 1) for j in range(chips)]
    ahead = jnp.int32(0)
    behind = jnp.int32(0)
    spot = jnp.int32(0)
    source_spot = jnp.int32(0)
    for j in range(chips):
        spot = jnp.where(chip == order[j], j, spot)
        source_spot = jnp.where(col == order[j], j, source_spot)
        ahead = jnp.where(chip == order[j], order[(j + 1) % chips], ahead)
        behind = jnp.where(chip == order[j], order[(j + chips - 1) % chips], behind)
    to_chip = jnp.where(core % 2 == 0, ahead, behind)
    to_row = to_chip * fan + core
    is_source = chip == col
    feeds_ring = to_chip != col
    turn = jnp.where(core % 2 == 0, spot - source_spot, source_spot - spot)
    ring_hops = (turn + chips) % chips

    def weight_copy(t):
        at = pl.ds(pl.multiple_of((t % per) * tw, tw), tw)
        return pltpu.make_async_copy(w_ref.at[:, at], wbuf.at[t % ring], w_sem.at[t % ring])

    def start_weights(s, carry):
        weight_copy(s).start()
        return carry

    res_copy = pltpu.make_async_copy(res_hbm, res_ref, in_sem.at[0])
    gain_copy = pltpu.make_async_copy(gain_hbm, gain, in_sem.at[1])
    early_copy = pltpu.make_async_copy(gram_in.at[pl.ds(0, early.shape[0])], early, in_sem.at[2])
    res_copy.start()
    gain_copy.start()
    lax.fori_loop(0, ring, start_weights, 0)

    barrier = pltpu.get_barrier_semaphore()
    for off in range(1, rows):
        pl.semaphore_signal(barrier, inc=1, device_id=((me + off) % rows, col), device_id_type=MESH)

    @pl.when(col > 0)
    def _():
        pl.semaphore_signal(barrier, inc=1, device_id=(me, col - 1), device_id_type=MESH)

    @pl.when(col < last)
    def _():
        pl.semaphore_signal(barrier, inc=1, device_id=(me, col + 1), device_id_type=MESH)

    pl.semaphore_wait(barrier, rows - 1 + jnp.minimum(col, 1) + jnp.minimum(last - col, 1))

    def piece(b, row):
        return attn.at[b, pl.ds(pl.multiple_of(row * PIECE, PIECE), PIECE)]

    def mine(b):
        return attn_ref.at[pl.ds(pl.multiple_of(b * PIECE, PIECE), PIECE)]

    def attn_local(b):
        return pltpu.make_async_copy(mine(b), piece(b, me), loc_sem.at[b])

    def attn_far(b, off):
        there = ((chip + off) % chips) * fan + core
        return remote(mine(b), piece(b, me), at_send.at[b, off], at_recv.at[b, me], there, col)

    def attn_mate(b, off, other):
        mate = chip * fan + (core + other) % fan
        slot = ((chip + chips - off) % chips) * fan + core
        src = mine(b) if off == 0 else piece(b, slot)
        return remote(src, piece(b, slot), at_fwd.at[b, off, other], at_recv.at[b, slot], mate, col)

    def attn_arrive(b, slot):
        remote(mine(b), piece(b, slot), at_send.at[b, 0], at_recv.at[b, slot], me, col).wait_recv()

    def attn_start(b):
        attn_local(b).start()
        for other in range(1, fan):
            attn_mate(b, 0, other).start()
        for off in range(1, chips):
            attn_far(b, off).start()

    def attn_forward(b):
        for off in range(1, chips):
            attn_arrive(b, ((chip + chips - off) % chips) * fan + core)
            for other in range(1, fan):
                attn_mate(b, off, other).start()

    def attn_finish(b):
        attn_local(b).wait()
        for off in range(chips):
            for other in range(1, fan):
                attn_arrive(b, ((chip + chips - off) % chips) * fan + (core + other) % fan)

    stats[me] = jnp.zeros(stats.shape[1:], f32)
    attn_start(0)
    res_copy.wait()
    gain_copy.wait()
    attn_forward(0)
    if blocks > 1:
        attn_start(1)

    def z_copy(d, i):
        nxt = jnp.minimum(col + 1, last) if d == 0 else jnp.maximum(col - 1, 0)
        return remote(z_out.at[d, i % SLOTS], z_in.at[d, i], z_send.at[d, i], z_recv.at[d, i], me, nxt)

    def zs_copy(d, i):
        nxt = jnp.minimum(col + 1, last) if d == 0 else jnp.maximum(col - 1, 0)
        return remote(zs_out.at[d, i], zs_in.at[d, i], zs_send.at[d, i], zs_recv.at[d, i], me, nxt)

    def z_decode(d, i):
        return root17(z_in[d, i]) * spread(zs_in[d, i], lanes_per, tw)

    def z_free(d, i):
        @pl.when(i >= SLOTS)
        def _():
            z_copy(d, i - SLOTS).wait_send()

    def z_encode(d, i, value):
        top = jnp.maximum(jnp.max(jnp.abs(value), axis=1, keepdims=True), TINY)
        z_out[d, i % SLOTS] = power17(value * (TOP / top)).astype(bf16)
        zs_out[d, i] = pack(top * (1.0 / TOP), 0)

    def z_start(d, i):
        zs_copy(d, i).start()
        z_copy(d, i).start()

    def z_arrive(d, i):
        zs_copy(d, i).wait_recv()
        z_copy(d, i).wait_recv()

    def lanes(which):
        return pl.ds(pl.multiple_of(which * 128, 128), 128)

    def ring_copy(i):
        return remote(cp.at[core, i], cp.at[core, i], ring_send.at[i], cp_recv.at[core, i], to_row, col)

    def mate_copy(i, other):
        mate = chip * fan + (core + other) % fan
        return remote(cp.at[core, i], cp.at[core, i], mate_send.at[other, i], cp_recv.at[core, i], mate, col)

    def cp_arrive(which, i):
        remote(cp.at[which, i], cp.at[which, i], ring_send.at[i], cp_recv.at[which, i], me, col).wait_recv()

    def stat_copy(b, off):
        return remote(stats.at[me, b], stats.at[me, b], st_send.at[off, b], st_recv.at[me, b], (me + off) % rows, col)

    def stat_arrive(b, off):
        there = (me + off) % rows
        remote(stats.at[there, b], stats.at[there, b], st_send.at[off, b], st_recv.at[there, b], me, col).wait_recv()

    far = jnp.maximum(col, last - col)
    inner = jnp.logical_and(col > 0, col < last)
    right_lag = max(per + 2, RING_HOP * (chips - 1) + 1)

    def combine(i):
        b, s = i // per, i % per

        @pl.when(col == 0)
        def _():
            gathered(i, b, s, own[i] + z_decode(1, i))

        @pl.when(inner)
        def _():
            gathered(i, b, s, own[i] + z_decode(0, i) + z_decode(1, i))

        @pl.when(col == last)
        def _():
            gathered(i, b, s, own[i] + z_decode(0, i))

        @pl.when(is_source)
        def _():
            ring_copy(i).start()
            for other in range(1, fan):
                mate_copy(i, other).start()

        @pl.when(s == per - 1)
        def _():
            for off in range(1, rows):
                stat_copy(b, off).start()

    def gathered(i, b, s, total):
        square = jnp.sum(total * total, axis=1, keepdims=True)
        stats[me, b] = jnp.where(s == 0, 0.0, stats[me, b]) + pack(square, s * lanes_per)
        st[i] = (total * gain[me * per + s]).T

        @pl.when(is_source)
        def _():
            cp[core, i] = power17(total * (lax.rsqrt(square + TINY) * TOP)).astype(bf16)

    def over_tiles(packed):
        shift = 64
        while shift >= lanes_per:
            packed = packed + pltpu.roll(packed, shift, axis=1)
            shift //= 2
        return packed

    def left(b):
        for off in range(1, rows):
            stat_arrive(b, off)
        total = stats[0, b]
        for r in range(1, rows):
            total = total + stats[r, b]
        panel = stats[col * fan, b]
        for k in range(1, fan):
            panel = panel + stats[col * fan + k, b]
        panel = over_tiles(panel) * (1.0 / (fan * per * tw)) + TINY
        level = lax.rsqrt(panel)
        for k in range(fan):
            cscale[k, b] = jnp.sqrt(stats[col * fan + k, b] + TINY) * level * (1.0 / TOP)
        weight = panel * level / (over_tiles(total) * (1.0 / model) + epsilon_norm)
        along = spread(weight, lanes_per, 128).T
        along = jnp.broadcast_to(along[:1, :], (tw, bt))
        here = pl.ds(pl.multiple_of(b * bt, bt), bt)
        there = pl.ds(pl.multiple_of(tokens + b * bt, bt), bt)

        def one(s, carry):
            value = st[b * per + s] * along
            high = value.astype(bf16)
            low = value - high.astype(f32)
            at = pl.ds(pl.multiple_of(s * tw, tw), tw)
            lt_hi[at, here] = high
            lt8[at, here] = value.astype(f8)
            lt8[at, there] = (low * LOW).astype(f8)
            return carry

        lax.fori_loop(0, per, one, 0)

    def right(i):
        b, s = i // per, i % per
        here = pl.ds(pl.multiple_of(b * bt, bt), bt)
        there = pl.ds(pl.multiple_of(tokens + b * bt, bt), bt)
        for other in range(1, fan):
            cp_arrive((core + other) % fan, i)
        for k in range(fan):
            scale = pltpu.roll(cscale[k, b], (128 - s * lanes_per) % 128, axis=1)
            value = root17(cp[k, i]) * spread(scale, lanes_per, tw) * gain[(col * fan + k) * per + s]
            high = value.astype(bf16)
            low = value - high.astype(f32)
            at = pl.ds(pl.multiple_of((k * per + s) * tw, tw), tw)
            r_hi[here, at] = high
            r8[here, at] = (low * LOW).astype(f8)
            r8[there, at] = value.astype(f8)

    def step(t, carry):
        @pl.when(t < tiles)
        def _():
            b, s = t // per, t % per

            @pl.when(s == 0)
            def _():
                attn_finish(b)

            weight_copy(t).wait()
            own[t] = jnp.dot(attn[b], wbuf[t % ring], preferred_element_type=f32)

            @pl.when(t + ring < tiles)
            def _():
                weight_copy(t + ring).start()

            @pl.when(t == per)
            def _():
                early_copy.start()

            at = pl.ds(pl.multiple_of(s * tw, tw), tw)
            g = (b * PIECE) // tile
            for f in range(fan):
                here = pl.ds(pl.multiple_of((col * fan + f) * PIECE, PIECE), PIECE)
                there = pl.ds(pl.multiple_of(f * tile + (b * PIECE) % tile, PIECE), PIECE)
                own[t, here, :] = own[t, here, :] + res_ref[g, there, at]

            @pl.when(jnp.logical_and(s == per // 2, b + 1 < blocks))
            def _():
                attn_forward(b + 1)

                @pl.when(b + 2 < blocks)
                def _():
                    attn_start(b + 2)

        up, down = t - HOP * col, t - HOP * (last - col)
        up_on = jnp.logical_and(up >= 0, up < tiles)
        down_on = jnp.logical_and(down >= 0, down < tiles)
        pair = jnp.logical_and(inner, jnp.logical_and(up_on, down_on))

        @pl.when(pair)
        def _():
            for d, i in ((0, up), (1, down)):
                z_free(d, i)
                z_arrive(d, i)
            values = [own[i] + z_decode(d, i) for d, i in ((0, up), (1, down))]
            for d, i in ((0, up), (1, down)):
                z_encode(d, i, values[d])
            for d, i in ((0, up), (1, down)):
                z_start(d, i)

        for d, i, on in ((0, up, up_on), (1, down, down_on)):
            first = col == (0 if d == 0 else last)
            end = col == (last if d == 0 else 0)

            @pl.when(jnp.logical_and(first, on))
            def _(d=d, i=i):
                z_free(d, i)
                z_encode(d, i, own[i])
                z_start(d, i)

            @pl.when(jnp.logical_and(end, on))
            def _(d=d, i=i):
                z_arrive(d, i)

            @pl.when(jnp.logical_and(jnp.logical_and(inner, on), jnp.logical_not(pair)))
            def _(d=d, i=i):
                z_free(d, i)
                z_arrive(d, i)
                z_encode(d, i, own[i] + z_decode(d, i))
                z_start(d, i)

        i = t - HOP * far

        @pl.when(jnp.logical_and(i >= 0, i < tiles))
        def _(i=i):
            combine(i)

        i = t - HOP * far - RING_HOP * ring_hops

        @pl.when(jnp.logical_and(ring_hops > 0, jnp.logical_and(i >= 0, i < tiles)))
        def _(i=i):
            cp_arrive(core, i)

            @pl.when(feeds_ring)
            def _():
                ring_copy(i).start()

            for other in range(1, fan):
                mate_copy(i, other).start()

        i = t - HOP * far - 2

        @pl.when(jnp.logical_and(i >= 0, jnp.logical_and(i < tiles, i % per == per - 1)))
        def _(i=i):
            left(i // per)

        i = t - HOP * far - right_lag

        @pl.when(jnp.logical_and(i >= 0, i < tiles))
        def _(i=i):
            right(i)

        return carry

    lax.fori_loop(0, tiles + HOP * far + right_lag, step, 0)

    early_copy.wait()

    def drain(i, carry):
        for other in range(1, fan):
            mate_copy(i, other).wait_send()

        @pl.when(jnp.logical_or(is_source, feeds_ring))
        def _():
            ring_copy(i).wait_send()

        for d in range(2):
            @pl.when(col != (last if d == 0 else 0))
            def _(d=d):
                zs_copy(d, i).wait_send()

                @pl.when(i >= tiles - SLOTS)
                def _():
                    z_copy(d, i).wait_send()
        return carry

    lax.fori_loop(0, tiles, drain, 0)

    def drain_block(b, carry):
        for off in range(1, rows):
            stat_copy(b, off).wait_send()
        for off in range(chips):
            for other in range(1, fan):
                attn_mate(b, off, other).wait_send()
        for off in range(1, chips):
            attn_far(b, off).wait_send()
        return carry

    lax.fori_loop(0, blocks, drain_block, 0)


def operands(attn, weights, residual, gain, gram_in, early, rows, cols, fan):
    own_tokens, depth = attn.shape
    width = weights.shape[1]
    model = width * rows
    blocks = own_tokens // PIECE
    bt = rows * PIECE
    tokens = blocks * bt
    per = 128 // (bt // 8)
    tw = width // per
    tiles = blocks * per
    chips = rows // fan
    vmem = pl.BlockSpec(memory_space=pltpu.VMEM)
    hbm = pl.BlockSpec(memory_space=pltpu.HBM)
    dma = pltpu.SemaphoreType.DMA
    return pl.pallas_call(
        functools.partial(operands_kernel, rows, cols, fan, model),
        out_shape=(
            jax.ShapeDtypeStruct((width, tokens), bf16),
            jax.ShapeDtypeStruct((width, 2 * tokens), f8),
            jax.ShapeDtypeStruct((tokens, fan * width), bf16),
            jax.ShapeDtypeStruct((2 * tokens, fan * width), f8),
            jax.ShapeDtypeStruct((early, gram_in.shape[1]), f32),
        ),
        in_specs=[hbm, hbm, hbm, hbm, hbm],
        out_specs=(vmem, vmem, vmem, vmem, vmem),
        scratch_shapes=[
            pltpu.VMEM(residual.shape, f32),
            pltpu.VMEM((rows * per, 1, tw), f32),
            pltpu.VMEM((blocks, bt, depth), bf16),
            pltpu.VMEM((WEIGHTS, depth, tw), bf16),
            pltpu.VMEM((tiles, bt, tw), f32),
            pltpu.VMEM((tiles, tw, bt), f32),
            pltpu.VMEM((2, SLOTS, bt, tw), bf16),
            pltpu.VMEM((2, tiles, bt, tw), bf16),
            pltpu.VMEM((2, tiles, 8, 128), f32),
            pltpu.VMEM((2, tiles, 8, 128), f32),
            pltpu.VMEM((fan, tiles, bt, tw), bf16),
            pltpu.VMEM((rows, blocks, 8, 128), f32),
            pltpu.VMEM((fan, blocks, 8, 128), f32),
            dma((WEIGHTS,)), dma((3,)), dma((blocks,)),
            dma((blocks, chips)), dma((blocks, chips, fan)), dma((blocks, rows)),
            dma((2, tiles)), dma((2, tiles)), dma((2, tiles)), dma((2, tiles)),
            dma((tiles,)), dma((fan, tiles)), dma((fan, tiles)),
            dma((rows, blocks)), dma((rows, blocks)),
        ],
        compiler_params=pltpu.CompilerParams(collective_id=0, has_side_effects=True, vmem_limit_bytes=31 << 20),
        name="operands",
    )(attn, weights, residual, gain.reshape(rows * per, 1, tw), gram_in)


def gram_kernel(tokens, step, lt_hi, lt8, r_hi, r8, early, gram_in, out, total, in_sem, out_sem):
    chunks, pieces = in_sem.shape
    height, width = total.shape[0] // chunks, total.shape[1] // pieces

    def window(c, p):
        return pl.ds(pl.multiple_of(c * height, height), height), pl.ds(p * width, width)

    def load(c, p):
        return pltpu.make_async_copy(gram_in.at[window(c, p)], total.at[window(c, p)], in_sem.at[c, p])

    def store(c, p):
        return pltpu.make_async_copy(total.at[window(c, p)], out.at[window(c, p)], out_sem.at[c, p])

    def start(c, carry):
        for p in range(pieces):
            load(c, p).start()
        return carry

    def product(c, p, begin):
        here = window(c, 0)[0]
        for j in range(width // step):
            at = slice(p * width + j * step, p * width + (j + 1) * step)
            low = jnp.dot(lt8[here, :], r8[:, at], preferred_element_type=f32)
            high = jnp.dot(lt_hi[here, :], r_hi[:, at], preferred_element_type=f32)
            total[here, at] = begin(here, at) + (high + low * (1.0 / LOW)) * (1.0 / tokens)
        store(c, p).start()

    def compute(c, carry):
        for p in range(pieces):
            load(c, p).wait()
            product(c, p, lambda here, at: total[here, at])
        return carry

    def finish(c, carry):
        for p in range(pieces):
            store(c, p).wait()
        return carry

    lax.fori_loop(1, chunks, start, 0)
    for p in range(pieces):
        product(0, p, lambda here, at: early[:, at])
    lax.fori_loop(1, chunks, compute, 0)
    lax.fori_loop(0, chunks, finish, 0)


def gram_product(lt_hi, lt8, r_hi, r8, early, gram_in):
    tokens = r_hi.shape[0]
    chunks, pieces = gram_in.shape[0] // HEIGHT, gram_in.shape[1] // 1024
    vmem = pl.BlockSpec(memory_space=pltpu.VMEM)
    hbm = pl.BlockSpec(memory_space=pltpu.HBM)
    return pl.pallas_call(
        functools.partial(gram_kernel, tokens, 256),
        out_shape=jax.ShapeDtypeStruct(gram_in.shape, f32),
        in_specs=[vmem, vmem, vmem, vmem, vmem, hbm],
        out_specs=hbm,
        scratch_shapes=[
            pltpu.VMEM(gram_in.shape, f32),
            pltpu.SemaphoreType.DMA((chunks, pieces)),
            pltpu.SemaphoreType.DMA((chunks, pieces)),
        ],
        compiler_params=pltpu.CompilerParams(vmem_limit_bytes=33 << 20),
        name="gram_product",
    )(lt_hi, lt8, r_hi, r8, early, gram_in)


def body(attn_out, o_weight, residual, norm_gain, gram_in):
    rows = lax.axis_size("row")
    cols = lax.axis_size("col")
    fan = rows // cols
    parts = operands(attn_out.reshape(-1, attn_out.shape[2]), o_weight, residual, norm_gain, gram_in, HEIGHT, rows, cols, fan)
    return gram_product(*parts, gram_in)


def solution(mesh):
    return jax.shard_map(
        body,
        mesh=mesh,
        in_specs=(
            P(None, "row", "col"),
            P("col", "row"),
            P(None, "col", "row"),
            P(),
            P("row", "col"),
        ),
        out_specs=P("row", "col"),
        check_vma=False,
    )
```
